128 devices in a mesh: row: 8 (over x, core), col: 16 (over z, y).
Axes of the slice: x: 4, y: 4, z: 4, core: 2. Of those that a mesh axis runs over, the one named last changes fastest.
Arguments:
- right_sides: bfloat16 [32768, 12288], P('row', 'col'), may hold values from -6 to 6
- factor_panels: bfloat16 [32768, 1024], P(('row', 'col')), may hold values from -0.1875 to 0.1875
- inverse_blocks: float32 [4, 256, 256], replicated, may hold values from -1 to 1, as said below
Outputs:
- solved_sides: float32 [32768, 12288], P('row', 'col')
The draws below stay inside these ranges and needn't reach their ends.
Inputs may be any that keep to these rules, and one draw needn't show every extreme that they name: `inverse_blocks`: each block is unit lower triangular.
All inputs are finite; a program needn't handle non-finite values.
Results may differ from the reference program's by a relative error of at most 0.003.
Values may be sent and summed in bfloat16 or wider, within the bound.
No kernel may reach another device: no remote copies, remote signals or barrier semaphores. Data moves between devices by JAX's collectives and lax.ppermute only.
A program may use at most 192 MiB of HBM per device.

```python
import jax
import jax.numpy as jnp
from jax import lax

BS = 256
PANELS = 4
MB_DEV = 16
NRHS_DEV = 768
NR = 32768
NRHS = 12288
N_COL = 16


def draw_inverse_blocks(key, part):
    strict_part = jnp.clip(jax.random.normal(key, (PANELS, BS, BS), jnp.float32), -4.0, 4.0)
    strict_part = strict_part / jnp.sqrt(jnp.float32(BS))
    below_mask = jnp.tril(jnp.ones((BS, BS), jnp.float32), -1)
    return strict_part * below_mask + jnp.eye(BS, dtype=jnp.float32)


def shard_levels(stream_key, dims, split, least, high):
    level, own = 1.0, jax.random.fold_in(stream_key, 6)
    for dim, parts in split:
        steps = jnp.exp(jax.random.uniform(jax.random.fold_in(own, dim), (parts,), jnp.float32, least / len(split), high / len(split)))
        level = level * jnp.repeat(steps, dims[dim] // parts).reshape([-1 if axis == dim else 1 for axis in range(len(dims))])
    return level


def scatter_about(own_key, extent, scale, most, shards=(), kind=jnp.bfloat16):
    gain = shard_levels(own_key, extent, shards, -0.22, 0.18) if shards else 1.0
    entries = jax.random.normal(own_key, extent, jnp.float32) * scale * gain
    return jnp.minimum(jnp.maximum(entries, -most), most).astype(kind)


def setup_inputs(seed: int = 0) -> dict:
    key_of = jax.random.split(jax.random.key(seed), 4)
    right_sides = scatter_about(key_of[0], (NR, NRHS), 1.0, 6.0, ((0, 8), (1, 16)))
    factor_panels = scatter_about(key_of[1], (NR, PANELS * BS), (PANELS * BS) ** -0.5, 0.1875, ((0, 128),))
    inverse_blocks = draw_inverse_blocks(jax.random.fold_in(key_of[3], 71), 0)
    return dict(right_sides=right_sides, factor_panels=factor_panels, inverse_blocks=inverse_blocks)


def solve_columns(column_group, factor_panels, inverse_blocks):
    current = column_group.astype(jnp.float32)
    factor = factor_panels.astype(jnp.float32)
    row_blocks = jnp.arange(NR, dtype=jnp.int32) // BS
    for panel_num in range(PANELS):
        offset = panel_num * MB_DEV * BS
        leading = lax.dynamic_slice_in_dim(current, offset, BS, 0)
        solved = jnp.dot(inverse_blocks[panel_num], leading, precision=lax.Precision.HIGHEST)
        rounded = lax.optimization_barrier(solved.astype(jnp.bfloat16))
        shared = rounded.astype(jnp.float32)
        update = jnp.dot(factor[:, panel_num * BS:(panel_num + 1) * BS], shared, precision=lax.Precision.HIGHEST)
        is_panel = (row_blocks % MB_DEV == 0) & (row_blocks // MB_DEV <= panel_num)
        current = current - jnp.where(is_panel[:, None], jnp.zeros_like(update), update)
        current = lax.dynamic_update_slice_in_dim(current, solved, offset, 0)
    return current


def reference(right_sides, factor_panels, inverse_blocks):
    groups = right_sides.reshape(NR, N_COL, NRHS_DEV).transpose(1, 0, 2)
    solved_groups = lax.map(lambda group_cols: solve_columns(group_cols, factor_panels, inverse_blocks), groups)
    return solved_groups.transpose(1, 0, 2).reshape(NR, NRHS)
```

```python
import functools

import jax
import jax.numpy as jnp
from jax import lax
from jax.experimental import pallas as pl
from jax.experimental.pallas import tpu as pltpu
from jax.sharding import PartitionSpec as P


BF = jnp.bfloat16
F32 = jnp.float32
HALF = 128
SIDE = 4


def y_perm(d):
    return [(z * 4 + y, z * 4 + (y + d) % 4) for z in range(4) for y in range(4)]


def z_perm(d):
    return [(z * 4 + y, ((z + d) % 4) * 4 + y) for z in range(4) for y in range(4)]


def x_perm(d, sources=(0, 1, 2, 3)):
    return [(x * 2 + k, ((x + d) % 4) * 2 + k) for x in sources for k in range(2)]


SWAP = [(r, r ^ 1) for r in range(8)]


def main_kernel(pieces, step, first, *refs):
    n_src = len(pieces)
    srcs = refs[:n_src]
    shared_ref, top_ref, rhs_ref = refs[n_src : n_src + 3]
    rest = refs[n_src + 3 :]
    if not first:
        rest = rest[1:]
    out_ref, lbuf, rbuf, obuf, offs, lsem, rsem, osem = rest
    flat = [p for src in pieces for p in src]
    total = len(flat)
    steps = total // step
    row = lax.axis_index("row")
    col = lax.axis_index("col")
    z, y = col // SIDE, col % SIDE
    at = 0
    for src_ref, src in zip(srcs, pieces):
        for i, (dz, dy, half) in enumerate(src):
            block = ((z + SIDE - dz) % SIDE) * SIDE + (y + SIDE - dy) % SIDE
            offs[at] = block * 2 + half
            s = at // step
            dst = pl.ds((at % step) * HALF, HALF)
            pltpu.make_async_copy(
                src_ref.at[pl.ds(i * HALF, HALF), :], lbuf.at[s, dst, :], lsem.at[s]
            ).start()
            start = pl.multiple_of((block * 2 + half) * HALF, HALF)
            pltpu.make_async_copy(
                rhs_ref.at[pl.ds(start, HALF), :], rbuf.at[s, dst, :], rsem.at[s]
            ).start()
            at += 1

    def body(s, carry):
        pltpu.make_async_copy(lbuf.at[s], lbuf.at[s], lsem.at[s]).wait()
        pltpu.make_async_copy(rbuf.at[s], rbuf.at[s], rsem.at[s]).wait()
        update = jnp.dot(lbuf[s], shared_ref[...], preferred_element_type=F32)
        obuf[s] = rbuf[s].astype(F32) - update
        for i in range(step):
            place = offs[s * step + i]

            @pl.when(jnp.logical_and(place < 2, row < 4))
            def _():
                begin = pl.multiple_of(place * HALF, HALF)
                obuf[s, pl.ds(i * HALF, HALF), :] = top_ref[pl.ds(begin, HALF), :]

        for i in range(step):
            place = offs[s * step + i]
            begin = pl.multiple_of(place * HALF, HALF)
            pltpu.make_async_copy(
                obuf.at[s, pl.ds(i * HALF, HALF), :],
                out_ref.at[pl.ds(begin, HALF), :],
                osem.at[s],
            ).start()
        return carry

    lax.fori_loop(0, steps, body, 0)

    def drain(s, carry):
        pltpu.make_async_copy(obuf.at[s], obuf.at[s], osem.at[s]).wait()
        return carry

    lax.fori_loop(0, steps, drain, 0)


def main_call(srcs, pieces, step, shared, top, rhs, out, name):
    total = sum(len(p) for p in pieces)
    steps = total // step
    rows, width = rhs.shape
    depth = shared.shape[0]
    first = out is None
    anywhere = pl.BlockSpec(memory_space=pl.ANY)
    vmem = pl.BlockSpec(memory_space=pltpu.VMEM)
    args = [*srcs, shared, top, rhs] + ([] if first else [out])
    specs = [anywhere] * len(srcs) + [vmem, vmem, anywhere] + ([] if first else [anywhere])
    return pl.pallas_call(
        functools.partial(main_kernel, pieces, step, first),
        out_shape=jax.ShapeDtypeStruct((rows, width), F32),
        in_specs=specs,
        out_specs=anywhere,
        input_output_aliases={} if first else {len(args) - 1: 0},
        scratch_shapes=[
            pltpu.VMEM((steps, step * HALF, depth), BF),
            pltpu.VMEM((steps, step * HALF, width), BF),
            pltpu.VMEM((steps, step * HALF, width), F32),
            pltpu.SMEM((total,), jnp.int32),
            pltpu.SemaphoreType.DMA((steps,)),
            pltpu.SemaphoreType.DMA((steps,)),
            pltpu.SemaphoreType.DMA((steps,)),
        ],
        compiler_params=pltpu.CompilerParams(vmem_limit_bytes=40 << 20),
        cost_estimate=pl.CostEstimate(
            flops=2 * total * HALF * depth * width,
            bytes_accessed=total * HALF * (depth * 2 + width * 6),
            transcendentals=0,
        ),
        name=name,
    )(*args)


def split(value):
    high = value.astype(BF)
    return high, (value - high.astype(F32)).astype(BF)


def dot(a, b):
    return jnp.dot(a, b, preferred_element_type=F32)


def solve_kernel(own_rows, other_rows, own_low, other_low, inverse_ref, shared_ref, top_ref, low):
    row = lax.axis_index("row")
    x, core = row // 2, row % 2
    size = inverse_ref.shape[1]
    quarter = size // SIDE
    for p in range(SIDE):
        slot = pl.multiple_of(((x + SIDE - p) % SIDE) * quarter, quarter)
        mine = own_low[pl.ds(slot, quarter), :]
        theirs = other_low[pl.ds(slot, quarter), :]
        low[0, p * quarter : (p + 1) * quarter, :] = jnp.where(core == 0, mine, theirs)
        low[1, p * quarter : (p + 1) * quarter, :] = jnp.where(core == 0, theirs, mine)
    for k in range(inverse_ref.shape[0]):
        lo = (k // 2) * size
        mine = own_rows[lo : lo + size, :]
        theirs = other_rows[lo : lo + size, :]
        current = jnp.where(core == k % 2, mine, theirs).astype(F32)
        if k:
            begin = 0 if k < 2 else size
            current -= dot(low[k % 2, :, begin : begin + k * size], shared_ref[: k * size, :])
        ih, il = split(inverse_ref[k])
        ch, cl = split(current)
        solved = dot(ih, ch) + (dot(ih, cl) + dot(il, ch))
        shared_ref[k * size : (k + 1) * size, :] = solved.astype(BF)

        @pl.when(row == k)
        def _():
            top_ref[...] = solved


def solve_call(own_rows, other_rows, own_low, other_low, inverse):
    panels, size, _ = inverse.shape
    width = own_rows.shape[1]
    vmem = pl.BlockSpec(memory_space=pltpu.VMEM)
    return pl.pallas_call(
        solve_kernel,
        out_shape=(
            jax.ShapeDtypeStruct((panels * size, width), BF),
            jax.ShapeDtypeStruct((size, width), F32),
        ),
        in_specs=[vmem] * 5,
        out_specs=(vmem, vmem),
        scratch_shapes=[pltpu.VMEM((2, size, 4 * size), BF)],
        compiler_params=pltpu.CompilerParams(vmem_limit_bytes=40 << 20),
        cost_estimate=pl.CostEstimate(
            flops=2 * 18 * size * size * width, bytes_accessed=6 << 20, transcendentals=0
        ),
        name="solve",
    )(own_rows, other_rows, own_low, other_low, inverse)


def pick(x, at0, at1, at2, at3):
    return jnp.where(x == 0, at0, jnp.where(x == 1, at1, jnp.where(x == 2, at2, at3)))


def per_device(right_sides, factor_panels, inverse_blocks):
    size = inverse_blocks.shape[1]
    quarter = size // SIDE
    row = lax.axis_index("row")
    col = lax.axis_index("col")
    x = row // 2
    z, y = col // SIDE, col % SIDE
    shift = lambda v, d: lax.ppermute(v, "col", y_perm(d))
    lift = lambda v, d: lax.ppermute(v, "col", z_perm(d))

    def quarter_of(chip):
        return lax.dynamic_slice(factor_panels, (quarter * chip, 0), (quarter, 3 * size))

    from0 = {0: quarter_of(x)}
    for d in (1, 3, 2):
        pairs = [(s * 16, t * 16) for s, t in x_perm(d, (0, 1))]
        from0[d] = lax.ppermute(quarter_of((x + d) % SIDE), ("row", "col"), pairs)
    first = pick(x, from0[0], from0[1], from0[2], from0[3])
    second = pick(x, from0[3], from0[0], from0[1], from0[2])
    low = jnp.concatenate([first[:, :size], second], axis=1)

    lead = right_sides[:size]
    got = {0: lead}
    for d in (1, 3, 2):
        got[d] = lax.ppermute(lead, "row", x_perm(d, (0, 1)))
    own_rows = jnp.concatenate(
        [pick(x, got[0], got[1], got[2], got[3]), pick(x, got[3], got[0], got[1], got[2])], 0
    )
    other_rows = lax.ppermute(own_rows, "row", SWAP)

    a, b = factor_panels[:HALF], factor_panels[HALF:]
    ya = {d: shift(a, d) for d in (1, 3, 2)}
    zb = {d: lift(b, d) for d in (1, 3, 2)}

    def spread(value, here, perm):
        parts = [lax.ppermute(value, "col", perm(d)) for d in (1, 3, 2)]
        return jnp.where(here == 0, value, parts[0] + parts[1] + parts[2])

    low = spread(low, y, lambda d: [(0, d)])
    low = spread(low, z, lambda d: [(k, d * 4 + k) for k in range(4)])

    yb = {d: shift(b, d) for d in (1, 3, 2)}
    za = {d: lift(a, d) for d in (1, 3, 2)}
    lows = [low] + [lax.ppermute(low, "row", x_perm(d)) for d in (1, 2, 3)]
    own_low = jnp.concatenate(lows, 0)
    other_low = lax.ppermute(own_low, "row", SWAP)

    pa = jnp.concatenate([ya[d] for d in (1, 3, 2)], 0)
    pb = jnp.concatenate([zb[d] for d in (1, 3, 2)], 0)
    zpa = {e: lift(pa, e) for e in (1, 3, 2)}
    ypb = {e: shift(pb, e) for e in (1, 3, 2)}

    shared, top = solve_call(own_rows, other_rows, own_low, other_low, inverse_blocks)

    srcs = [factor_panels, pa, pb]
    pieces = [
        [(0, 0, 0), (0, 0, 1)],
        [(0, d, 0) for d in (1, 3, 2)],
        [(d, 0, 1) for d in (1, 3, 2)],
    ]
    for d in (1, 3, 2):
        srcs += [yb[d], za[d]]
        pieces += [[(0, d, 1)], [(d, 0, 0)]]
    out = main_call(srcs, pieces, 2, shared, top, right_sides, None, "near")

    for e in (1, 3, 2):
        srcs = [zpa[e], ypb[e]]
        pieces = [[(e, d, 0) for d in (1, 3, 2)], [(d, e, 1) for d in (1, 3, 2)]]
        out = main_call(srcs, pieces, 3, shared, top, right_sides, out, "far%d" % e)
    return out


def solution(mesh):
    placed = (P("row", "col"), P(("row", "col"), None), P())
    return jax.shard_map(
        per_device, mesh=mesh, in_specs=placed, out_specs=P("row", "col"), check_vma=False
    )
```

```python
import jax
import jax.numpy as jnp
from jax import lax
from jax.experimental import pallas as pl
from jax.experimental.pallas import tpu as pltpu
from jax.sharding import PartitionSpec as P


BF = jnp.bfloat16
F32 = jnp.float32
SIDE = 4
RING = 4
STEPS = (1, 3, 2)
BOTH = ("row", "col")


def y_to(c, d):
    return (c // SIDE) * SIDE + (c % SIDE + d) % SIDE


def z_to(c, d):
    return (c // SIDE + d) % SIDE * SIDE + c % SIDE


def plane_perm(d, turned):
    return [
        (r * 16 + c, r * 16 + (z_to if r % 2 != turned else y_to)(c, d))
        for r in range(8)
        for c in range(16)
    ]


def x_perm(move):
    return [(x * 2 + k, move(x) * 2 + k) for x in range(SIDE) for k in range(2)]


SWAP = [(r, r ^ 1) for r in range(8)]


def dot(a, b):
    return jnp.dot(a, b, preferred_element_type=F32)


def main_kernel(*refs):
    own = refs[0]
    near, turned, far = refs[1:4], refs[4:7], refs[7:10]
    shared_ref, top_ref, rhs_ref, out_ref, obuf, osem = refs[10:]
    size = own.shape[0]
    row, col = lax.axis_index("row"), lax.axis_index("col")
    z, y = col // SIDE, col % SIDE
    core = lax.rem(row, 2)

    def emit(slot, factor, along, across):
        dy = jnp.where(core == 0, along, across)
        dz = jnp.where(core == 0, across, along)
        if slot >= RING:
            pltpu.make_async_copy(obuf.at[0], obuf.at[0], osem.at[slot % RING]).wait()
        slot = slot % RING
        block = lax.rem(z + SIDE - dz, SIDE) * SIDE + lax.rem(y + SIDE - dy, SIDE)
        begin = pl.multiple_of(block * size, size)
        obuf[slot] = rhs_ref[pl.ds(begin, size), :].astype(F32) - dot(factor, shared_ref[...])

        @pl.when(jnp.logical_and(block == 0, row < 4))
        def _():
            obuf[slot] = top_ref[...]

        pltpu.make_async_copy(
            obuf.at[slot], out_ref.at[pl.ds(begin, size), :], osem.at[slot]
        ).start()

    emit(0, own[...], 0, 0)
    for i, d in enumerate(STEPS):
        emit(1 + i, near[i][...], d, 0)
        emit(4 + i, turned[i][...], 0, d)
    for i, e in enumerate(STEPS):
        for j, d in enumerate(STEPS):
            emit(7 + 3 * i + j, far[i][j * size : (j + 1) * size, :], d, e)
    for slot in range(RING):
        pltpu.make_async_copy(obuf.at[slot], obuf.at[slot], osem.at[slot]).wait()


def main_call(own, near, turned, far, shared, top, rhs):
    rows, width = rhs.shape
    size, depth = own.shape
    vmem = pl.BlockSpec(memory_space=pltpu.VMEM)
    args = [own, *near, *turned, *far, shared, top, rhs]
    return pl.pallas_call(
        main_kernel,
        out_shape=jax.ShapeDtypeStruct((rows, width), F32),
        in_specs=[vmem] * len(args),
        out_specs=pl.BlockSpec(memory_space=pl.ANY),
        scratch_shapes=[
            pltpu.VMEM((RING, size, width), F32),
            pltpu.SemaphoreType.DMA((RING,)),
        ],
        compiler_params=pltpu.CompilerParams(vmem_limit_bytes=24 << 20),
        cost_estimate=pl.CostEstimate(
            flops=2 * rows * depth * width, bytes_accessed=rows * width * 4, transcendentals=0
        ),
        name="update",
    )(*args)


def split(value):
    high = value.astype(BF)
    return high, (value - high.astype(F32)).astype(BF)


def solve_kernel(*refs):
    own_rows, other_rows = refs[0:2], refs[2:4]
    own_low, other_low = refs[4:8], refs[8:12]
    inverse_ref, shared_ref, top_ref, low = refs[12:]
    row = lax.axis_index("row")
    x, core = row // 2, lax.rem(row, 2)
    size = inverse_ref.shape[1]
    quarter = size // SIDE
    for i, d in enumerate((0, *STEPS)):
        place = pl.multiple_of(lax.rem(x + SIDE - d, SIDE) * quarter, quarter)
        mine, theirs = own_low[i][...], other_low[i][...]
        low[0, pl.ds(place, quarter), :] = jnp.where(core == 0, mine, theirs)
        low[1, pl.ds(place, quarter), :] = jnp.where(core == 0, theirs, mine)
    outer = jnp.logical_or(x == 0, x == 3)
    for k in range(inverse_ref.shape[0]):
        here = outer if k < 2 else jnp.logical_not(outer)
        mine = jnp.where(here, own_rows[0][...], own_rows[1][...])
        theirs = jnp.where(here, other_rows[0][...], other_rows[1][...])
        current = jnp.where(core == k % 2, mine, theirs).astype(F32)
        if k:
            begin = 0 if k < 2 else size
            current -= dot(low[k % 2, :, begin : begin + k * size], shared_ref[: k * size, :])
        ih, il = split(inverse_ref[k])
        ch, cl = split(current)
        solved = dot(ih, ch) + (dot(ih, cl) + dot(il, ch))
        shared_ref[k * size : (k + 1) * size, :] = solved.astype(BF)

        @pl.when(row == k)
        def _():
            top_ref[...] = solved


def solve_call(own_rows, other_rows, own_low, other_low, inverse):
    panels, size, _ = inverse.shape
    width = own_rows[0].shape[1]
    vmem = pl.BlockSpec(memory_space=pltpu.VMEM)
    args = [*own_rows, *other_rows, *own_low, *other_low, inverse]
    return pl.pallas_call(
        solve_kernel,
        out_shape=(
            jax.ShapeDtypeStruct((panels * size, width), BF),
            jax.ShapeDtypeStruct((size, width), F32),
        ),
        in_specs=[vmem] * len(args),
        out_specs=(vmem, vmem),
        scratch_shapes=[pltpu.VMEM((2, size, 4 * size), BF)],
        compiler_params=pltpu.CompilerParams(vmem_limit_bytes=12 << 20),
        cost_estimate=pl.CostEstimate(
            flops=2 * 18 * size * size * width, bytes_accessed=6 << 20, transcendentals=0
        ),
        name="solve",
    )(*args)


def pick(index, at0, at1, at2, at3):
    return jnp.where(
        index == 0, at0, jnp.where(index == 1, at1, jnp.where(index == 2, at2, at3))
    )


def per_device(right_sides, factor_panels, inverse_blocks):
    size = inverse_blocks.shape[1]
    quarter = size // SIDE
    row = lax.axis_index("row")
    col = lax.axis_index("col")
    x, core = row // 2, row % 2
    z, y = col // SIDE, col % SIDE

    def along(value, d):
        return lax.ppermute(value, BOTH, plane_perm(d, 0))

    def across(value, d):
        return lax.ppermute(value, BOTH, plane_perm(d, 1))

    def over_x(value, move):
        return lax.ppermute(value, "row", x_perm(move))

    def swap(value):
        return lax.ppermute(value, "row", SWAP)

    def quarter_of(chip):
        return lax.dynamic_slice(factor_panels, (quarter * chip, 0), (quarter, 3 * size))

    got = {0: quarter_of(x)}
    for d in STEPS:
        got[d] = over_x(quarter_of((x + d) % SIDE), lambda s: (s + d) % SIDE)
    first = pick(x, got[0], got[1], got[2], got[3])
    second = pick(x, got[3], got[0], got[1], got[2])
    low = jnp.concatenate([first[:, :size], second], axis=1)

    near = [along(factor_panels, d) for d in STEPS]
    lead = right_sides[:size]
    passed = over_x(lead, lambda s: 3 - s)

    spot = jnp.where(core == 0, z, y)
    parts = {d: across(low, d) for d in STEPS}
    low = pick(spot, low, parts[1], parts[2], parts[3])
    turned = [across(factor_panels, d) for d in STEPS]
    spot = jnp.where(core == 0, y, z)
    parts = {d: along(low, d) for d in STEPS}
    low = pick(spot, low, parts[1], parts[2], parts[3])

    mine = jnp.where(x < 2, lead, passed)
    theirs = over_x(mine, lambda s: s ^ 1)
    own_rows = [mine, theirs]
    other_rows = [swap(mine), swap(theirs)]

    far = [across(jnp.concatenate(near, 0), e) for e in STEPS]

    own_low = [low] + [over_x(low, lambda s: (s + d) % SIDE) for d in STEPS]
    other_low = [swap(v) for v in own_low]

    shared, top = solve_call(own_rows, other_rows, own_low, other_low, inverse_blocks)
    return main_call(factor_panels, near, turned, far, shared, top, right_sides)


def solution(mesh):
    placed = (P("row", "col"), P(BOTH, None), P())

    return jax.shard_map(
        per_device, mesh=mesh, in_specs=placed, out_specs=P("row", "col"), check_vma=False
    )
```

```python
import functools

import jax
import jax.numpy as jnp
from jax import lax
from jax.experimental import pallas as pl
from jax.experimental.pallas import tpu as pltpu
from jax.sharding import PartitionSpec as P


BF = jnp.bfloat16
F32 = jnp.float32
SIDE = 4
RING = 3
HALF = 128
LIMIT = 28
STEPS = (1, 3, 2)
BOTH = ("row", "col")


def y_to(c, d):
    return (c // SIDE) * SIDE + (c % SIDE + d) % SIDE


def z_to(c, d):
    return (c // SIDE + d) % SIDE * SIDE + c % SIDE


def plane_perm(d, turned):
    return [
        (r * 16 + c, r * 16 + (z_to if r % 2 != turned else y_to)(c, d))
        for r in range(8)
        for c in range(16)
    ]


def x_perm(move):
    return [(x * 2 + k, move(x) * 2 + k) for x in range(SIDE) for k in range(2)]


SWAP = [(r, r ^ 1) for r in range(8)]


def dot(a, b):
    return jnp.dot(a, b, preferred_element_type=F32)


def update_kernel(tiles, first, *refs):
    n_src = 1 + max(src for src, _, _ in tiles)
    srcs = refs[:n_src]
    shared_ref, top_ref, rhs_ref = refs[n_src : n_src + 3]
    out_ref, obuf, osem, lbuf, lsem = refs[n_src + 3 + (not first) :]
    size = top_ref.shape[0]
    row, col = lax.axis_index("row"), lax.axis_index("col")
    z, y = col // SIDE, col % SIDE
    core = lax.rem(row, 2)

    def fetch(t):
        src, start, pieces = tiles[t]
        rows = sum(count for count, _, _, _ in pieces)
        return pltpu.make_async_copy(
            srcs[src].at[pl.ds(start, rows)], lbuf.at[t, pl.ds(0, rows)], lsem.at[t]
        )

    for t in range(len(tiles)):
        fetch(t).start()

    def finish(t):
        rows = sum(count for count, _, _, _ in tiles[t][2])
        part = obuf.at[t % RING, pl.ds(0, rows)]
        pltpu.make_async_copy(part, part, osem.at[t % RING]).wait()

    for t, (_, _, pieces) in enumerate(tiles):
        if t >= RING:
            finish(t - RING)
        slot = t % RING
        rows = sum(count for count, _, _, _ in pieces)
        fetch(t).wait()
        product = dot(lbuf[t, :rows, :], shared_ref[...])
        at = 0
        for count, along, across, offset in pieces:
            dy = jnp.where(core == 0, along, across)
            dz = jnp.where(core == 0, across, along)
            block = lax.rem(z + SIDE - dz, SIDE) * SIDE + lax.rem(y + SIDE - dy, SIDE)
            begin = pl.multiple_of(block * size + offset, HALF)
            right = rhs_ref[pl.ds(begin, count), :].astype(F32)
            obuf[slot, at : at + count, :] = right - product[at : at + count]

            @pl.when(jnp.logical_and(block == 0, row < 4))
            def _():
                obuf[slot, at : at + count, :] = top_ref[offset : offset + count, :]

            pltpu.make_async_copy(
                obuf.at[slot, pl.ds(at, count)], out_ref.at[pl.ds(begin, count)], osem.at[slot]
            ).start()
            at += count
    for t in range(max(0, len(tiles) - RING), len(tiles)):
        finish(t)


def update_call(srcs, tiles, shared, top, rhs, out):
    rows, width = rhs.shape
    depth = shared.shape[0]
    first = out is None
    vmem = pl.BlockSpec(memory_space=pltpu.VMEM)
    anywhere = pl.BlockSpec(memory_space=pl.ANY)
    args = [*srcs, shared, top, rhs] + ([] if first else [out])
    specs = [anywhere] * len(srcs) + [vmem] * 3 + ([] if first else [anywhere])
    tallest = max(sum(p[0] for p in pieces) for _, _, pieces in tiles)
    total = sum(p[0] for _, _, pieces in tiles for p in pieces)
    return pl.pallas_call(
        functools.partial(update_kernel, tiles, first),
        out_shape=jax.ShapeDtypeStruct((rows, width), F32),
        in_specs=specs,
        out_specs=anywhere,
        input_output_aliases={} if first else {len(args) - 1: 0},
        scratch_shapes=[
            pltpu.VMEM((RING, tallest, width), F32),
            pltpu.SemaphoreType.DMA((RING,)),
            pltpu.VMEM((len(tiles), tallest, depth), BF),
            pltpu.SemaphoreType.DMA((len(tiles),)),
        ],
        compiler_params=pltpu.CompilerParams(vmem_limit_bytes=LIMIT << 20),
        cost_estimate=pl.CostEstimate(
            flops=2 * total * depth * width, bytes_accessed=total * width * 4, transcendentals=0
        ),
    )(*args)


def split(value):
    high = value.astype(BF)
    return high, (value - high.astype(F32)).astype(BF)


def solve_kernel(*refs):
    own_rows, other_rows = refs[0:2], refs[2:4]
    own_low, other_low = refs[4:8], refs[8:12]
    inverse_hbm, shared_ref, top_ref, low, inverse_ref, sem = refs[12:]
    copies = []
    for k in range(inverse_hbm.shape[0]):
        copies.append(
            pltpu.make_async_copy(inverse_hbm.at[k], inverse_ref.at[k], sem.at[k])
        )
        copies[k].start()
    row = lax.axis_index("row")
    x, core = row // 2, lax.rem(row, 2)
    size = inverse_ref.shape[1]
    quarter = size // SIDE
    for i, d in enumerate((0, *STEPS)):
        place = pl.multiple_of(lax.rem(x + SIDE - d, SIDE) * quarter, quarter)
        mine, theirs = own_low[i][...], other_low[i][...]
        low[0, pl.ds(place, quarter), :] = jnp.where(core == 0, mine, theirs)
        low[1, pl.ds(place, quarter), :] = jnp.where(core == 0, theirs, mine)
    outer = jnp.logical_or(x == 0, x == 3)
    for k in range(inverse_ref.shape[0]):
        here = outer if k < 2 else jnp.logical_not(outer)
        mine = jnp.where(here, own_rows[0][...], own_rows[1][...])
        theirs = jnp.where(here, other_rows[0][...], other_rows[1][...])
        current = jnp.where(core == k % 2, mine, theirs).astype(F32)
        if k:
            begin = 0 if k < 2 else size
            current -= dot(low[k % 2, :, begin : begin + k * size], shared_ref[: k * size, :])
        copies[k].wait()
        ih, il = split(inverse_ref[k])
        ch, cl = split(current)
        both = dot(jnp.concatenate([ih, il], 0), ch)
        solved = both[:size] + (dot(ih, cl) + both[size:])
        shared_ref[k * size : (k + 1) * size, :] = solved.astype(BF)

        @pl.when(row == k)
        def _():
            top_ref[...] = solved


def solve_call(own_rows, other_rows, own_low, other_low, inverse):
    panels, size, _ = inverse.shape
    width = own_rows[0].shape[1]
    vmem = pl.BlockSpec(memory_space=pltpu.VMEM)
    args = [*own_rows, *other_rows, *own_low, *other_low, inverse]
    return pl.pallas_call(
        solve_kernel,
        out_shape=(
            jax.ShapeDtypeStruct((panels * size, width), BF),
            jax.ShapeDtypeStruct((size, width), F32),
        ),
        in_specs=[vmem] * (len(args) - 1) + [pl.BlockSpec(memory_space=pltpu.HBM)],
        out_specs=(vmem, vmem),
        scratch_shapes=[
            pltpu.VMEM((2, size, 4 * size), BF),
            pltpu.VMEM((panels, size, size), F32),
            pltpu.SemaphoreType.DMA((panels,)),
        ],
        compiler_params=pltpu.CompilerParams(vmem_limit_bytes=12 << 20),
        cost_estimate=pl.CostEstimate(
            flops=2 * 18 * size * size * width, bytes_accessed=6 << 20, transcendentals=0
        ),
        name="solve",
    )(*args)


def copy_kernel(n_src, moves, *refs):
    outs, sem = refs[n_src:-1], refs[-1]
    copies = [
        pltpu.make_async_copy(
            refs[src].at[pl.ds(start, rows)], outs[dst].at[pl.ds(to, rows)], sem.at[i]
        )
        for i, (src, start, rows, dst, to) in enumerate(moves)
    ]
    for copy in copies:
        copy.start()
    for copy in copies:
        copy.wait()


def copy_call(srcs, moves, out_rows):
    width = srcs[0].shape[1]
    count = len(out_rows)
    return pl.pallas_call(
        functools.partial(copy_kernel, len(srcs), moves),
        out_shape=[jax.ShapeDtypeStruct((rows, width), BF) for rows in out_rows],
        in_specs=[pl.BlockSpec(memory_space=pl.ANY)] * len(srcs),
        out_specs=[pl.BlockSpec(memory_space=pltpu.VMEM)] * count,
        scratch_shapes=[pltpu.SemaphoreType.DMA((len(moves),))],
        compiler_params=pltpu.CompilerParams(vmem_limit_bytes=4 << 20),
        cost_estimate=pl.CostEstimate(
            flops=0, bytes_accessed=4 * sum(out_rows) * width, transcendentals=0
        ),
    )(*srcs)


def pick(index, at0, at1, at2, at3):
    return jnp.where(
        index == 0, at0, jnp.where(index == 1, at1, jnp.where(index == 2, at2, at3))
    )


def per_device(right_sides, factor_panels, inverse_blocks):
    size = inverse_blocks.shape[1]
    quarter = size // SIDE
    row = lax.axis_index("row")
    col = lax.axis_index("col")
    x, core = row // 2, row % 2
    z, y = col // SIDE, col % SIDE

    def along(value, d):
        return lax.ppermute(value, BOTH, plane_perm(d, 0))

    def across(value, d):
        return lax.ppermute(value, BOTH, plane_perm(d, 1))

    def over_x(value, move):
        return lax.ppermute(value, "row", x_perm(move))

    def swap(value):
        return lax.ppermute(value, "row", SWAP)

    def quarter_of(chip):
        return lax.dynamic_slice(factor_panels, (quarter * chip, 0), (quarter, 3 * size))

    got = {0: quarter_of(x)}
    for d in STEPS:
        got[d] = over_x(quarter_of((x + d) % SIDE), lambda s: (s + d) % SIDE)
    first = pick(x, got[0], got[1], got[2], got[3])
    second = pick(x, got[3], got[0], got[1], got[2])
    low = jnp.concatenate([first[:, :size], second], axis=1)

    near = [along(factor_panels, d) for d in STEPS]
    lead = right_sides[:size]
    passed = over_x(lead, lambda s: 3 - s)

    spot = jnp.where(core == 0, z, y)
    parts = {d: across(low, d) for d in STEPS}
    low = pick(spot, low, parts[1], parts[2], parts[3])
    turned = [across(factor_panels, d) for d in STEPS]
    spot = jnp.where(core == 0, y, z)
    parts = {d: along(low, d) for d in STEPS}
    low = pick(spot, low, parts[1], parts[2], parts[3])

    mine = jnp.where(x < 2, lead, passed)
    theirs = over_x(mine, lambda s: s ^ 1)
    own_rows = [mine, theirs]
    other_rows = [swap(mine), swap(theirs)]

    stack = jnp.concatenate(near, 0)
    far = {e: across(stack, e) for e in (1, 3)}
    part = 3 * HALF
    moves = [(0, 0, part, 0, 0), (1, part, part, 1, 0)]
    upper, lower = copy_call([far[1], far[3]], moves, [part, part])
    beyond = [across(upper, 1), across(lower, 3)]

    own_low = [low] + [over_x(low, lambda s: (s + d) % SIDE) for d in STEPS]
    other_low = [swap(v) for v in own_low]

    shared, top = solve_call(own_rows, other_rows, own_low, other_low, inverse_blocks)

    def halves(e):
        one, three, two = ((d, e) for d in STEPS)
        return [
            [(size, *one, 0), (HALF, *three, 0)],
            [(HALF, *three, HALF), (size, *two, 0)],
        ]

    tiles = [(0, 0, [(size, 0, 0, 0)])]
    tiles += [(1, i * 3 * HALF, p) for i, p in enumerate(halves(0))]
    tiles += [(2 + i, 0, [(size, 0, d, 0)]) for i, d in enumerate(STEPS)]
    tiles += [(5, i * part, p) for i, p in enumerate(halves(1))]
    tiles += [(6, i * part, p) for i, p in enumerate(halves(3))]
    srcs = [factor_panels, stack, *turned, far[1], far[3]]
    out = update_call(srcs, tiles, shared, top, right_sides, None)
    tiles = [(i, 0, p) for i, p in enumerate(halves(2))]
    return update_call(beyond, tiles, shared, top, right_sides, out)


def solution(mesh):
    placed = (P("row", "col"), P(BOTH, None), P())

    return jax.shard_map(
        per_device, mesh=mesh, in_specs=placed, out_specs=P("row", "col"), check_vma=False
    )
```

```python
import functools

import jax
import jax.numpy as jnp
from jax import lax
from jax.experimental import pallas as pl
from jax.experimental.pallas import tpu as pltpu
from jax.sharding import PartitionSpec as P


BF = jnp.bfloat16
F32 = jnp.float32
SIDE = 4
RING = 3
HALF = 128
LIMIT = 28
STEPS = (1, 3, 2)
BOTH = ("row", "col")


def y_to(c, d):
    return (c // SIDE) * SIDE + (c % SIDE + d) % SIDE


def z_to(c, d):
    return (c // SIDE + d) % SIDE * SIDE + c % SIDE


def plane_perm(d, turned):
    return [
        (r * 16 + c, r * 16 + (z_to if r % 2 != turned else y_to)(c, d))
        for r in range(8)
        for c in range(16)
    ]


def x_perm(move):
    return [(x * 2 + k, move(x) * 2 + k) for x in range(SIDE) for k in range(2)]


SWAP = [(r, r ^ 1) for r in range(8)]


def dot(a, b):
    return jnp.dot(a, b, preferred_element_type=F32)


def tile_rows(tile):
    return sum(count for _, _, pieces in tile for count, _, _, _ in pieces)


def update_kernel(tiles, direct, first, *refs):
    n_src = 1 + max(src for tile in tiles for src, _, _ in tile)
    srcs = refs[:n_src]
    shared_ref, top_ref, rhs_ref = refs[n_src : n_src + 3]
    out_ref, obuf, osem, lbuf, lsem = refs[n_src + 3 + (not first) :]
    size = top_ref.shape[0]
    row, col = lax.axis_index("row"), lax.axis_index("col")
    z, y = col // SIDE, col % SIDE
    core = lax.rem(row, 2)

    for t, tile in enumerate(tiles):
        to = 0
        for src, start, pieces in tile if tile[0][0] not in direct else ():
            rows = sum(count for count, _, _, _ in pieces)
            pltpu.make_async_copy(
                srcs[src].at[pl.ds(start, rows)], lbuf.at[t, pl.ds(to, rows)], lsem.at[t]
            ).start()
            to += rows

    def finish(t):
        rows = tile_rows(tiles[t])
        part = obuf.at[t % RING, pl.ds(0, rows)]
        pltpu.make_async_copy(part, part, osem.at[t % RING]).wait()

    for t, tile in enumerate(tiles):
        if t >= RING:
            finish(t - RING)
        slot = t % RING
        rows = tile_rows(tile)
        if tile[0][0] in direct:
            factor = srcs[tile[0][0]][...]
        else:
            whole = lbuf.at[t, pl.ds(0, rows)]
            pltpu.make_async_copy(whole, whole, lsem.at[t]).wait()
            factor = lbuf[t, :rows, :]
        product = dot(factor, shared_ref[...])
        places = []
        at = 0
        for count, along, across, offset in (p for _, _, ps in tile for p in ps):
            dy = jnp.where(core == 0, along, across)
            dz = jnp.where(core == 0, across, along)
            block = lax.rem(z + SIDE - dz, SIDE) * SIDE + lax.rem(y + SIDE - dy, SIDE)
            begin = pl.multiple_of(block * size + offset, HALF)
            right = rhs_ref[pl.ds(begin, count), :].astype(F32)
            obuf[slot, at : at + count, :] = right - product[at : at + count]
            places.append((at, count, block, offset, begin))
            at += count
        for at, count, block, offset, begin in places:

            @pl.when(jnp.logical_and(block == 0, row < 4))
            def _():
                obuf[slot, at : at + count, :] = top_ref[offset : offset + count, :]

            pltpu.make_async_copy(
                obuf.at[slot, pl.ds(at, count)], out_ref.at[pl.ds(begin, count)], osem.at[slot]
            ).start()
    for t in range(max(0, len(tiles) - RING), len(tiles)):
        finish(t)


def update_call(srcs, tiles, direct, shared, top, rhs, out):
    rows, width = rhs.shape
    depth = shared.shape[0]
    first = out is None
    vmem = pl.BlockSpec(memory_space=pltpu.VMEM)
    anywhere = pl.BlockSpec(memory_space=pl.ANY)
    args = [*srcs, shared, top, rhs] + ([] if first else [out])
    specs = [vmem if i in direct else anywhere for i in range(len(srcs))] + [vmem] * 3 + ([] if first else [anywhere])
    tallest = max(tile_rows(tile) for tile in tiles)
    total = sum(tile_rows(tile) for tile in tiles)
    return pl.pallas_call(
        functools.partial(update_kernel, tiles, direct, first),
        out_shape=jax.ShapeDtypeStruct((rows, width), F32),
        in_specs=specs,
        out_specs=anywhere,
        input_output_aliases={} if first else {len(args) - 1: 0},
        scratch_shapes=[
            pltpu.VMEM((RING, tallest, width), F32),
            pltpu.SemaphoreType.DMA((RING,)),
            pltpu.VMEM((len(tiles), tallest, depth), BF),
            pltpu.SemaphoreType.DMA((len(tiles),)),
        ],
        compiler_params=pltpu.CompilerParams(vmem_limit_bytes=LIMIT << 20),
        cost_estimate=pl.CostEstimate(
            flops=2 * total * depth * width, bytes_accessed=total * width * 4, transcendentals=0
        ),
    )(*args)


def split(value):
    high = value.astype(BF)
    return high, (value - high.astype(F32)).astype(BF)


def solve_kernel(*refs):
    own_rows, other_rows = refs[0:2], refs[2:4]
    own_low, other_low = refs[4:8], refs[8:12]
    inverse_hbm, shared_ref, top_ref, low, inverse_ref, sem = refs[12:]
    copies = []
    for k in range(inverse_hbm.shape[0]):
        copies.append(
            pltpu.make_async_copy(inverse_hbm.at[k], inverse_ref.at[k], sem.at[k])
        )
        copies[k].start()
    row = lax.axis_index("row")
    x, core = row // 2, lax.rem(row, 2)
    size = inverse_ref.shape[1]
    quarter = size // SIDE
    for i, d in enumerate((0, *STEPS)):
        place = pl.multiple_of(lax.rem(x + SIDE - d, SIDE) * quarter, quarter)
        mine, theirs = own_low[i][...], other_low[i][...]
        low[0, pl.ds(place, quarter), :] = jnp.where(core == 0, mine, theirs)
        low[1, pl.ds(place, quarter), :] = jnp.where(core == 0, theirs, mine)
    outer = jnp.logical_or(x == 0, x == 3)
    for k in range(inverse_ref.shape[0]):
        here = outer if k < 2 else jnp.logical_not(outer)
        mine = jnp.where(here, own_rows[0][...], own_rows[1][...])
        theirs = jnp.where(here, other_rows[0][...], other_rows[1][...])
        current = jnp.where(core == k % 2, mine, theirs).astype(F32)
        if k:
            begin = 0 if k < 2 else size
            current -= dot(low[k % 2, :, begin : begin + k * size], shared_ref[: k * size, :])
        copies[k].wait()
        ih, il = split(inverse_ref[k])
        ch, cl = split(current)
        both = dot(jnp.concatenate([ih, il], 0), ch)
        solved = both[:size] + (dot(ih, cl) + both[size:])
        shared_ref[k * size : (k + 1) * size, :] = solved.astype(BF)

        @pl.when(row == k)
        def _():
            top_ref[...] = solved


def solve_call(own_rows, other_rows, own_low, other_low, inverse):
    panels, size, _ = inverse.shape
    width = own_rows[0].shape[1]
    vmem = pl.BlockSpec(memory_space=pltpu.VMEM)
    args = [*own_rows, *other_rows, *own_low, *other_low, inverse]
    return pl.pallas_call(
        solve_kernel,
        out_shape=(
            jax.ShapeDtypeStruct((panels * size, width), BF),
            jax.ShapeDtypeStruct((size, width), F32),
        ),
        in_specs=[vmem] * (len(args) - 1) + [pl.BlockSpec(memory_space=pltpu.HBM)],
        out_specs=(vmem, vmem),
        scratch_shapes=[
            pltpu.VMEM((2, size, 4 * size), BF),
            pltpu.VMEM((panels, size, size), F32),
            pltpu.SemaphoreType.DMA((panels,)),
        ],
        compiler_params=pltpu.CompilerParams(vmem_limit_bytes=12 << 20),
        cost_estimate=pl.CostEstimate(
            flops=2 * 18 * size * size * width, bytes_accessed=6 << 20, transcendentals=0
        ),
        name="solve",
    )(*args)


def copy_kernel(n_src, moves, *refs):
    outs, sem = refs[n_src:-1], refs[-1]
    copies = [
        pltpu.make_async_copy(
            refs[src].at[pl.ds(start, rows)], outs[dst].at[pl.ds(to, rows)], sem.at[i]
        )
        for i, (src, start, rows, dst, to) in enumerate(moves)
    ]
    for copy in copies:
        copy.start()
    for copy in copies:
        copy.wait()


def copy_call(srcs, moves, out_rows):
    width = srcs[0].shape[1]
    count = len(out_rows)
    return pl.pallas_call(
        functools.partial(copy_kernel, len(srcs), moves),
        out_shape=[jax.ShapeDtypeStruct((rows, width), BF) for rows in out_rows],
        in_specs=[pl.BlockSpec(memory_space=pl.ANY)] * len(srcs),
        out_specs=[pl.BlockSpec(memory_space=pltpu.VMEM)] * count,
        scratch_shapes=[pltpu.SemaphoreType.DMA((len(moves),))],
        compiler_params=pltpu.CompilerParams(vmem_limit_bytes=4 << 20),
        cost_estimate=pl.CostEstimate(
            flops=0, bytes_accessed=4 * sum(out_rows) * width, transcendentals=0
        ),
    )(*srcs)


def pick(index, at0, at1, at2, at3):
    return jnp.where(
        index == 0, at0, jnp.where(index == 1, at1, jnp.where(index == 2, at2, at3))
    )


def per_device(right_sides, factor_panels, inverse_blocks):
    size = inverse_blocks.shape[1]
    quarter = size // SIDE
    row = lax.axis_index("row")
    col = lax.axis_index("col")
    x, core = row // 2, row % 2
    z, y = col // SIDE, col % SIDE

    def along(value, d):
        return lax.ppermute(value, BOTH, plane_perm(d, 0))

    def across(value, d):
        return lax.ppermute(value, BOTH, plane_perm(d, 1))

    def over_x(value, move):
        return lax.ppermute(value, "row", x_perm(move))

    def swap(value):
        return lax.ppermute(value, "row", SWAP)

    def quarter_of(chip):
        return lax.dynamic_slice(factor_panels, (quarter * chip, 0), (quarter, 3 * size))

    got = {0: quarter_of(x)}
    for d in STEPS:
        got[d] = over_x(quarter_of((x + d) % SIDE), lambda s: (s + d) % SIDE)
    first = pick(x, got[0], got[1], got[2], got[3])
    second = pick(x, got[3], got[0], got[1], got[2])
    low = jnp.concatenate([first[:, :size], second], axis=1)

    near = [along(factor_panels, d) for d in STEPS]
    lead = right_sides[:size]
    passed = over_x(lead, lambda s: 3 - s)

    spot = jnp.where(core == 0, z, y)
    parts = {d: across(low, d) for d in STEPS}
    low = pick(spot, low, parts[1], parts[2], parts[3])
    turned = [across(factor_panels, d) for d in STEPS]
    spot = jnp.where(core == 0, y, z)
    parts = {d: along(low, d) for d in STEPS}
    low = pick(spot, low, parts[1], parts[2], parts[3])

    mine = jnp.where(x < 2, lead, passed)
    theirs = over_x(mine, lambda s: s ^ 1)
    own_rows = [mine, theirs]
    other_mine = swap(mine)
    other_rows = [other_mine, swap(theirs)]

    stack = jnp.concatenate(near, 0)
    far = {e: across(stack, e) for e in (1, 3)}
    part = 3 * HALF
    moves = [(0, 0, part, 0, 0), (1, part, part, 1, 0)]
    upper, lower = copy_call([far[1], far[3]], moves, [part, part])
    beyond = [across(upper, 1), across(lower, 3)]

    own_low = [low] + [over_x(low, lambda s: (s + d) % SIDE) for d in STEPS]
    other_low = [swap(own_low[0])]
    for d, value in zip(STEPS, own_low[1:]):
        other_low.append(swap(value))

    shared, top = solve_call(own_rows, other_rows, own_low, other_low, inverse_blocks)

    def row_of(src, e):
        return (src, 0, [(size, d, e, 0) for d in STEPS])

    tiles = [
        [(0, 0, [(size, 0, 0, 0)])],
        [(2, 0, [(size, 0, 1, 0)])],
        [(3, 0, [(size, 0, 3, 0)])],
        [(4, 0, [(size, 0, 2, 0)])],
        [row_of(1, 0)],
        [row_of(5, 1)],
        [row_of(6, 3)],
    ]
    srcs = [factor_panels, stack, *turned, far[1], far[3]]
    out = update_call(srcs, tiles, (0, 2, 3, 4), shared, top, right_sides, None)
    one, three, two = ((d, 2) for d in STEPS)
    tiles = [
        [(0, 0, [(size, *one, 0), (HALF, *three, 0)])],
        [(1, 0, [(HALF, *three, HALF), (size, *two, 0)])],
    ]
    return update_call(beyond, tiles, (0, 1), shared, top, right_sides, out)


def solution(mesh):
    placed = (P("row", "col"), P(BOTH, None), P())

    return jax.shard_map(
        per_device, mesh=mesh, in_specs=placed, out_specs=P("row", "col"), check_vma=False
    )
```
